32 devices in a mesh: grp: 8 (over y, x, core), sub: 4 (over z).
Axes of the slice: x: 2, y: 2, z: 4, core: 2. Of those that a mesh axis runs over, the one named last changes fastest.
Arguments:
- blocks: bfloat16 [256, 128, 128], P(('grp', 'sub')), may hold values from -0.5 to 0.5
- block_cols: int32 [256], P(('grp', 'sub')), may hold values from 0 to 31, as said below
- far_slots: int32 [32, 32], P(('grp', 'sub')), may hold values from 0 to 7, as said below
- pair_lists: int32 [32, 4, 128], P(('grp', 'sub')), may hold values from 0 to 7, as said below
Outputs:
- participation: float32 [4096], P(('grp', 'sub'))
- total: float32 [], replicated
The draws below stay inside these ranges and needn't reach their ends.
Inputs may be any that keep to these rules, and one draw needn't show every extreme that they name: `block_cols`: the block column of slot t is at most its block row t // 8. `far_slots`: the 4 slots of one block row and source group are distinct. `pair_lists`: rows 0 and 2 hold slot numbers below 8, row 1 positions below 4, row 3 holds 0 or 1; within one block row and source group no two triples share both their left slot and far position.
All inputs are finite; a program needn't handle non-finite values.
Results may differ from the reference program's by a relative error of at most 0.00035.
Values may be sent and summed in bfloat16 or wider, within the bound.
No kernel may reach another device: no remote copies, remote signals or barrier semaphores. Data moves between devices by JAX's collectives and lax.ppermute only.
A program may use at most 64 MiB of HBM per device.

```python
import math
import jax
import jax.numpy as jnp
from jax import lax

BS = 128
KD = 8
FAR = 4
P_SIZE = 16
GROUPS = 8
ROWBLOCKS = 32
N_SUB = 4


def draw_block_cols(key, part):
    owners = jnp.arange(ROWBLOCKS * KD, dtype=jnp.int32) // KD
    first = jax.random.fold_in(key, 11)
    second = jax.random.fold_in(key, 12)
    diagonal = jax.random.randint(first, (ROWBLOCKS * KD,), 0, 3) == 0
    spread = jax.random.randint(second, (ROWBLOCKS * KD,), 0, owners + 1)
    return jnp.where(diagonal, owners, spread).astype(jnp.int32)


def build_lists(key):
    base = jax.random.fold_in(key, 30)
    width = GROUPS * P_SIZE
    scores = jax.random.randint(jax.random.fold_in(base, 1), (ROWBLOCKS, GROUPS, KD), 0, 2 ** 20) * KD
    scores = scores + jnp.arange(KD, dtype=jnp.int32)
    order = jnp.argsort(scores, axis=-1, stable=True).astype(jnp.int32)
    chosen_far = order[:, :, :FAR].reshape(ROWBLOCKS, GROUPS * FAR)
    pairs = FAR * KD
    pair_scores = jax.random.randint(jax.random.fold_in(base, 2), (ROWBLOCKS, GROUPS, pairs), 0, 2 ** 16) * pairs
    pair_scores = pair_scores + jnp.arange(pairs, dtype=jnp.int32)
    picked = jnp.argsort(pair_scores, axis=-1, stable=True).astype(jnp.int32)[:, :, :P_SIZE]
    left_slot = picked % KD
    far_place = picked // KD
    mask_slot = jax.random.randint(jax.random.fold_in(base, 3), (ROWBLOCKS, GROUPS, P_SIZE), 0, KD)
    triples = jnp.stack([left_slot, far_place, mask_slot], axis=1).reshape(ROWBLOCKS, 3, width)
    source = jnp.arange(width, dtype=jnp.int32) // P_SIZE
    bound = 4 * GROUPS - 3 * source
    draws = jax.random.randint(jax.random.fold_in(base, 4), (ROWBLOCKS, 1, width), 0, 4 * GROUPS)
    live = (draws < bound[None, None, :]).astype(jnp.int32)
    lists = jnp.concatenate([triples.astype(jnp.int32), live], axis=1)
    return (chosen_far.astype(jnp.int32), lists)


def draw_far_slots(key, part):
    return build_lists(key)[0]


def draw_pair_lists(key, part):
    return build_lists(key)[1]


def shard_levels(key, dims, split, least, top_value):
    gain = 1.0
    for axis_at, parts in split:
        steps = jax.random.uniform(jax.random.fold_in(jax.random.fold_in(key, 6), axis_at), (parts,), jnp.float32, least / len(split), top_value / len(split))
        gain = gain * jnp.repeat(jnp.exp(steps), dims[axis_at] // parts).reshape((-1,) + (1,) * (len(dims) - 1 - axis_at))
    return gain


def centred(key, dims, scale, most, pieces=(), held_as=jnp.bfloat16):
    entries = scale * jax.random.normal(key, dims, jnp.float32)
    if pieces:
        entries = entries * shard_levels(key, dims, pieces, -0.22, 0.18)
    return jnp.clip(entries, -most, most).astype(held_as)


def setup_inputs(seed: int = 0) -> dict:
    splits = jax.random.split(jax.random.key(seed), 5)
    blocks = centred(splits[0], (ROWBLOCKS * KD, BS, BS), 0.07, 0.5, ((0, 32),))
    block_cols = draw_block_cols(jax.random.fold_in(splits[4], 71), 0)
    far_slots = draw_far_slots(jax.random.fold_in(splits[4], 71), 0)
    pair_lists = draw_pair_lists(jax.random.fold_in(splits[4], 71), 0)
    return {"blocks": blocks, "block_cols": block_cols, "far_slots": far_slots, "pair_lists": pair_lists}


def reference(blocks, block_cols, far_slots, pair_lists):
    count = blocks.shape[0]
    size = blocks.shape[1]
    owners = jnp.arange(count, dtype=jnp.int32) // KD
    inner = jnp.arange(size, dtype=jnp.int32)
    strict = inner[:, None] > inner[None, :]
    on_diag = block_cols == owners
    masked = jnp.where(on_diag[:, None, None] & jnp.logical_not(strict)[None], 0.0, blocks.astype(jnp.float32))
    columns = jnp.arange(GROUPS * P_SIZE, dtype=jnp.int32)

    def one_row(row):
        lists = pair_lists[row]
        sub_index = row % N_SUB
        group_of = columns // P_SIZE
        source = group_of * N_SUB + sub_index
        far_slot = far_slots[row][group_of * FAR + lists[1]]
        left = masked[row * KD + lists[0]]
        far = masked[source * KD + far_slot]
        mask = masked[row * KD + lists[2]]
        product = jnp.einsum('wik,wkj->wij', left, far)
        sums = lax.optimization_barrier(jnp.sum(mask * product, axis=2))
        return lax.optimization_barrier(jnp.sum(lists[3].astype(jnp.float32)[:, None] * sums, axis=0))
    rows = lax.map(one_row, jnp.arange(ROWBLOCKS, dtype=jnp.int32))
    participation = rows.reshape(ROWBLOCKS * size)
    total = jnp.sum(participation) / math.sqrt(ROWBLOCKS * size)
    return (participation, total)
```

```python
import functools
import itertools
import math

import jax
import jax.numpy as jnp
from jax import lax
from jax.experimental import pallas as pl
from jax.experimental.pallas import tpu as pltpu
from jax.sharding import PartitionSpec as P


class Places:
    def __init__(self, count):
        self.count = count
        self.cycle = 4 if count % 4 == 0 else count
        self.mids = count // self.cycle

    def split(self, place):
        if self.cycle != 4:
            return (place, 0)
        low = place % 2
        high = place // (2 * self.mids)
        turn = 2 * low + high * (3 - 4 * low)
        return (turn, (place // 2) % self.mids)

    def join(self, turn, mid):
        if self.cycle != 4:
            return turn
        return (turn % 2) * 2 * self.mids + mid * 2 + ((turn + 1) // 2) % 2

    def step(self, place, by):
        turn, mid = self.split(place)
        return self.join((turn + by[0]) % self.cycle, (mid + by[1]) % self.mids)

    def gap(self, there, here):
        return ((there[0] - here[0]) % self.cycle, (there[1] - here[1]) % self.mids)

    def cover(self):
        steps = sorted(
            itertools.product(range(self.cycle), range(self.mids)),
            key=lambda s: ((s[0] > 0) + (s[1] > 0), s),
        )

        def reached(chosen):
            return {self.gap(a, b) for a in chosen for b in chosen}

        chosen = [(0, 0)]
        while len(reached(chosen)) < self.count:
            chosen.append(max(steps, key=lambda s: len(reached(chosen + [s]))))
        near = (self.cycle // 2, 0) if self.cycle == 4 else None
        held = [s for s in chosen if s in ((0, 0), near)] + [s for s in chosen if s not in ((0, 0), near)]
        pairs = {}
        for (i, row), (j, source) in itertools.product(enumerate(held), enumerate(held)):
            wanted = self.gap(source, row)
            if wanted not in pairs or max(i, j) < max(pairs[wanted]):
                pairs[wanted] = (i, j)
        early = sum(1 for s in held if s in ((0, 0), near))
        return held, sorted(pairs.values()), early


def fill_kept(places, step, raw, meta, kept, keep, subs):
    stored = raw.shape[0]
    me = places.step(lax.axis_index("grp"), step) * subs + lax.axis_index("sub")
    for slot in range(stored):
        on_diag = (meta[5, slot] == me).astype(jnp.int32)
        kept[slot] = raw[slot] * keep[on_diag]
    kept[stored] = jnp.zeros_like(kept[stored])


def fill_keep(keep):
    size = keep.shape[1]
    rows = lax.broadcasted_iota(jnp.int32, (size, size), 0)
    columns = lax.broadcasted_iota(jnp.int32, (size, size), 1)
    keep[0] = jnp.ones((size, size), keep.dtype)
    keep[1] = (rows > columns).astype(jnp.float32).astype(keep.dtype)


def add_triples(acc, row, source, meta, group, groups):
    nothing = row.shape[0] - 1
    width = meta.shape[1] // groups
    named = meta.far_width // groups
    ref = meta.ref
    for w in range(width):
        at = group * width + w
        far = ref[4, group * named + ref[1, at]]
        mask = jnp.where(ref[3, at] == 1, ref[2, at], nothing)
        product = jnp.dot(row[ref[0, at]], source[far], preferred_element_type=jnp.float32)
        acc = acc + row[mask].astype(jnp.float32) * product
    return acc


class Meta:
    def __init__(self, ref, far_width):
        self.ref = ref
        self.shape = ref.shape
        self.far_width = far_width


def along_lanes(acc):
    return jnp.sum(acc.T, axis=0, keepdims=True)


def pair_sums(places, groups, far_width, held, pairs, metas, kept):
    sums = {}
    me = lax.axis_index("grp")
    for i, members in itertools.groupby(pairs, key=lambda p: p[0]):
        size = kept[i].shape[1]
        acc = jnp.zeros((size, size), jnp.float32)
        for _, j in members:
            group = places.step(me, held[j])
            acc = add_triples(acc, kept[i], kept[j], Meta(metas[i], far_width), group, groups)
        sums[i] = along_lanes(acc)
    return sums


def early_kernel(places, groups, subs, far_width, held, pairs, count, *refs):
    metas, raws = refs[:count], refs[count : 2 * count]
    kept, sums_out, keep = refs[2 * count : 3 * count], refs[3 * count], refs[3 * count + 1]
    fill_keep(keep)
    for i in range(count):
        fill_kept(places, held[i], raws[i], metas[i], kept[i], keep, subs)
    sums = pair_sums(places, groups, far_width, held, pairs, metas, kept)
    sums_out[...] = jnp.zeros_like(sums_out)
    for i, vector in sums.items():
        sums_out[i : i + 1, :] = vector


def late_kernel(places, groups, subs, far_width, held, pairs, early, *refs):
    count = len(held)
    metas = refs[:count]
    near = refs[count : count + early]
    raws = refs[count + early : 2 * count]
    before, out, keep = refs[2 * count], refs[2 * count + 1], refs[2 * count + 2]
    late = refs[2 * count + 3 :]
    fill_keep(keep)
    kept = list(near) + list(late)
    for i in range(early, count):
        fill_kept(places, held[i], raws[i - early], metas[i], kept[i], keep, subs)
    sums = pair_sums(places, groups, far_width, held, pairs, metas, kept)
    for i in range(early):
        sums[i] = before[i : i + 1, :] + sums[i] if i in sums else before[i : i + 1, :]
    size = keep.shape[1]
    total = sum(sums.values())
    out[:, :, :size] = jnp.zeros((out.shape[0], 1, size), out.dtype)
    out[:, :, size:] = jnp.broadcast_to(total[None], (out.shape[0], 1, size))
    for i, vector in sums.items():
        owner = places.step(lax.axis_index("grp"), held[i]) * subs + lax.axis_index("sub")
        out[owner, :, :size] = vector


def local(blocks, block_cols, far_slots, pair_lists):
    stored, size = blocks.shape[:2]
    groups = lax.axis_size("grp")
    subs = lax.axis_size("sub")
    width = pair_lists.shape[2]
    far_width = far_slots.shape[1]
    places = Places(groups)
    held, pairs, early = places.cover()

    def brought(array, step):
        if step == (0, 0):
            return array
        return lax.ppermute(array, "grp", [(places.step(g, step), g) for g in range(groups)])

    raws = [brought(blocks, step) for step in held]
    meta = jnp.concatenate(
        [
            pair_lists[0],
            jnp.pad(far_slots, ((0, 0), (0, width - far_width))),
            jnp.pad(block_cols[None], ((0, 0), (0, width - stored))),
        ],
        axis=0,
    )
    metas = [brought(meta, step) for step in held]

    smem = pl.BlockSpec(memory_space=pltpu.SMEM)
    vmem = pl.BlockSpec(memory_space=pltpu.VMEM)
    kept_shape = (stored + 1, size, size)
    keep = pltpu.VMEM((2, size, size), blocks.dtype)
    early_pairs = [p for p in pairs if max(p) < early]
    late_pairs = [p for p in pairs if max(p) >= early]
    block_flops = 2 * size * size * size * (width // groups)

    def cost(count, arrays):
        return pl.CostEstimate(
            flops=count * block_flops, bytes_accessed=arrays * stored * size * size * 2, transcendentals=0
        )

    *near, before = pl.pallas_call(
        functools.partial(early_kernel, places, groups, subs, far_width, held, early_pairs, early),
        out_shape=[jax.ShapeDtypeStruct(kept_shape, blocks.dtype)] * early
        + [jax.ShapeDtypeStruct((8 * (-(-early // 8)), size), jnp.float32)],
        in_specs=[smem] * early + [vmem] * early,
        out_specs=[vmem] * (early + 1),
        scratch_shapes=[keep],
        cost_estimate=cost(len(early_pairs), 2 * early),
        name="early",
    )(*metas[:early], *raws[:early])
    sent = pl.pallas_call(
        functools.partial(late_kernel, places, groups, subs, far_width, held, late_pairs, early),
        out_shape=jax.ShapeDtypeStruct((groups * subs, 1, 2 * size), jnp.float32),
        in_specs=[smem] * len(held) + [vmem] * (len(held) + 1),
        out_specs=vmem,
        scratch_shapes=[keep] + [pltpu.VMEM(kept_shape, blocks.dtype)] * (len(held) - early),
        cost_estimate=cost(len(late_pairs), len(held)),
        name="late",
    )(*metas, *near, *raws[early:], before)
    received = lax.all_to_all(sent, ("grp", "sub"), split_axis=0, concat_axis=0, tiled=True)
    summed = jnp.sum(received, axis=(0, 1))
    total = jnp.sum(summed[size:]) / math.sqrt(groups * subs * size)
    return (summed[:size], total)


def solution(mesh):
    placed = (
        P(("grp", "sub"), None, None),
        P(("grp", "sub")),
        P(("grp", "sub"), None),
        P(("grp", "sub"), None, None),
    )
    return jax.shard_map(
        local, mesh=mesh, in_specs=placed, out_specs=(P(("grp", "sub")), P()), check_vma=False
    )
```

```python
import functools
import itertools
import math

import jax
import jax.numpy as jnp
from jax import lax
from jax.experimental import pallas as pl
from jax.experimental.pallas import tpu as pltpu
from jax.sharding import PartitionSpec as P

FIELD = 8


class Places:
    def __init__(self, count):
        self.count = count
        self.cycle = 4 if count % 4 == 0 else count
        self.mids = count // self.cycle

    def split(self, place):
        if self.cycle != 4:
            return (place, 0)
        low = place % 2
        high = place // (2 * self.mids)
        turn = 2 * low + high * (3 - 4 * low)
        return (turn, (place // 2) % self.mids)

    def join(self, turn, mid):
        if self.cycle != 4:
            return turn
        return (turn % 2) * 2 * self.mids + mid * 2 + ((turn + 1) // 2) % 2

    def step(self, place, by):
        turn, mid = self.split(place)
        return self.join((turn + by[0]) % self.cycle, (mid + by[1]) % self.mids)

    def gap(self, there, here):
        return ((there[0] - here[0]) % self.cycle, (there[1] - here[1]) % self.mids)

    def cover(self):
        steps = sorted(
            itertools.product(range(self.cycle), range(self.mids)),
            key=lambda s: ((s[0] > 0) + (s[1] > 0), s),
        )

        def reached(chosen):
            return {self.gap(a, b) for a in chosen for b in chosen}

        chosen = [(0, 0)]
        while len(reached(chosen)) < self.count:
            chosen.append(max(steps, key=lambda s: len(reached(chosen + [s]))))
        held = sorted(chosen, key=lambda s: (s != (0, 0), s != (2, 0), s))
        pairs = {}
        for (i, row), (j, source) in itertools.product(enumerate(held), enumerate(held)):
            wanted = self.gap(source, row)
            if wanted not in pairs or max(i, j) < max(pairs[wanted]):
                pairs[wanted] = (i, j)
        return held, sorted(pairs.values())


class Plan:
    def __init__(self, groups, subs, width, far_width):
        self.groups = groups
        self.subs = subs
        self.listed = width // groups
        self.named = far_width // groups
        self.places = Places(groups)
        self.held, self.pairs = self.places.cover()
        self.near = 2 if (2, 0) in self.held and len(self.held) > 2 else 1
        self.order = sorted(range(len(self.held)), key=lambda i: (self.held[i] == (2, 0), i))

    def group(self, i):
        return self.places.step(lax.axis_index("grp"), self.held[i])

    def owner(self, i):
        return self.group(i) * self.subs + lax.axis_index("sub")


def pack_kernel(plan, pair_lists, far_slots, block_cols, raw, meta, strict, kept):
    groups, listed, named = plan.groups, plan.listed, plan.named
    stored, size = raw.shape[:2]
    left, place, mask, live = (pair_lists[0, field : field + 1] for field in range(4))
    width = place.shape[1]
    spread = lax.broadcasted_iota(jnp.int32, (groups * named, width), 0)
    source = lax.broadcasted_iota(jnp.int32, (groups * named, width), 1) // listed
    wanted = (spread == source * named + place).astype(jnp.float32)
    slots = jnp.broadcast_to(far_slots[...].astype(jnp.float32), (8, groups * named))
    far = jnp.dot(slots, wanted, preferred_element_type=jnp.float32)[:1].astype(jnp.int32)
    codes = left + far * 2**FIELD + jnp.where(live == 1, mask, stored) * 4**FIELD
    for group in range(groups):
        meta[group, :, :listed] = codes[:, group * listed : (group + 1) * listed]
    for slot in range(stored):
        meta[groups + slot] = jnp.full((1, size), block_cols[slot] != plan.owner(0), meta.dtype)
    rows = lax.broadcasted_iota(jnp.int32, (size, size), 0)
    columns = lax.broadcasted_iota(jnp.int32, (size, size), 1)
    strict[...] = (rows > columns).astype(jnp.float32).astype(strict.dtype)
    keep_strict(groups, raw, meta, strict, kept)


def keep_strict(groups, raw, meta, strict, kept, wide=None):
    stored = raw.shape[0]
    for slot in range(stored):
        off_diag = meta[groups + slot].astype(jnp.float32).astype(kept.dtype)
        kept[slot] = raw[slot] * jnp.maximum(strict[...], off_diag)
        if wide is not None:
            wide[slot] = kept[slot].astype(wide.dtype)
    kept[stored] = jnp.zeros_like(kept[stored])
    if wide is not None:
        wide[stored] = jnp.zeros_like(wide[stored])


def add_triples(plan, acc, row, masks, source, codes):
    field = 2**FIELD - 1
    for w in range(plan.listed):
        code = codes[0, w]
        left = row[code & field]
        far = source[(code >> FIELD) & field]
        mask = masks[code >> (2 * FIELD)]
        acc = acc + mask.astype(jnp.float32) * jnp.dot(left, far, preferred_element_type=jnp.float32)
    return acc


def stage_kernel(plan, first, last, new, pairs, *refs):
    refs = list(refs)
    strict = refs.pop(0)
    metas = [refs.pop(0) for _ in range(new.stop)]
    kept = [refs.pop(0) for _ in range(new.start)]
    raws = [refs.pop(0) for _ in new]
    before = None if first else refs.pop(0)
    if not last:
        kept += [refs.pop(0) for _ in new]
    out = refs.pop(0)
    if last:
        kept += [refs.pop(0) for _ in new]

    for i in new:
        keep_strict(plan.groups, raws[i - new.start], metas[i], strict, kept[i])
    size = kept[0].shape[1]
    done = 0 if first else new.start
    sums = {}
    for i in range(new.stop):
        acc = before[i] if i < done else jnp.zeros((size, size), jnp.float32)
        for row, j in pairs:
            if row == i:
                acc = add_triples(plan, acc, kept[i], kept[i], kept[j], metas[i][plan.group(j)])
        if last:
            sums[i] = jnp.sum(acc.T, axis=0, keepdims=True)
        else:
            out[i] = acc
    if not last:
        return
    out[:, :, :size] = jnp.zeros((out.shape[0], 1, size), out.dtype)
    out[:, :, size:] = jnp.broadcast_to(sum(sums.values())[None], (out.shape[0], 1, size))
    for i, vector in sums.items():
        out[plan.owner(i), :, :size] = vector


def last_kernel(divisor, received, participation, total):
    size = participation.shape[0]
    summed = jnp.sum(received[:, 0, :], axis=0, keepdims=True)
    participation[...] = summed[0, :size]
    total[0] = jnp.sum(summed[:, size:]) / divisor


def in_vmem(array):
    return pltpu.with_memory_space_constraint(array, pltpu.VMEM)


def local(blocks, block_cols, far_slots, pair_lists):
    stored, size = blocks.shape[:2]
    groups = lax.axis_size("grp")
    subs = lax.axis_size("sub")
    width = pair_lists.shape[2]
    far_width = far_slots.shape[1]
    plan = Plan(groups, subs, width, far_width)
    held = plan.held

    def brought(array, i):
        if i == 0:
            return array
        pairs = [(plan.places.step(g, held[i]), g) for g in range(groups)]
        return lax.ppermute(array, "grp", pairs)

    raws = {i: brought(blocks, i) for i in plan.order}
    kept_shape = (stored + 1, size, size)
    own_vmem = pltpu.CompilerParams(vmem_limit_bytes=16 * 2**20)
    smem = pl.BlockSpec(memory_space=pltpu.SMEM)
    vmem = pl.BlockSpec(memory_space=pltpu.VMEM)
    meta, strict, own = pl.pallas_call(
        functools.partial(pack_kernel, plan),
        out_shape=[
            pltpu.VMEM((groups + stored, 1, size), jnp.int32),
            pltpu.VMEM((size, size), blocks.dtype),
            pltpu.VMEM(kept_shape, blocks.dtype),
        ],
        in_specs=[vmem, vmem, smem, vmem],
        out_specs=[vmem, vmem, vmem],
        compiler_params=own_vmem,
        name="pack",
    )(pair_lists, far_slots, block_cols, blocks)
    metas = {i: brought(meta, i) for i in plan.order}

    stages = [range(1, plan.near)] + [range(i, i + 1) for i in range(plan.near, len(held))]
    kept = [own]
    sums = []
    for at, new in enumerate(stages):
        first, last = at == 0, at == len(stages) - 1
        pairs = [p for p in plan.pairs if max(p) in new or first and max(p) == 0]
        if last:
            out_shape = pltpu.VMEM((groups * subs, 1, 2 * size), jnp.float32)
        else:
            out_shape = [pltpu.VMEM(kept_shape, blocks.dtype)] * len(new)
            out_shape += [pltpu.VMEM((new.stop, size, size), jnp.float32)]
        operands = [in_vmem(a) for a in [strict] + [metas[i] for i in range(new.stop)] + kept + [raws[i] for i in new] + sums]
        call = pl.pallas_call(
            functools.partial(stage_kernel, plan, first, last, new, pairs),
            out_shape=out_shape,
            in_specs=[vmem] * len(operands),
            out_specs=vmem if last else [vmem] * (len(new) + 1),
            scratch_shapes=[pltpu.VMEM(kept_shape, blocks.dtype)] * len(new) if last else [],
            cost_estimate=pl.CostEstimate(
                flops=len(pairs) * plan.listed * 2 * size**3,
                bytes_accessed=2 * len(new) * stored * size * size * blocks.dtype.itemsize,
                transcendentals=0,
            ),
            compiler_params=own_vmem,
        )
        out = call(*operands)
        if not last:
            kept += out[:-1]
            sums = [out[-1]]
    received = in_vmem(lax.all_to_all(out, ("grp", "sub"), split_axis=0, concat_axis=0, tiled=True))
    participation, total = pl.pallas_call(
        functools.partial(last_kernel, math.sqrt(groups * subs * size)),
        out_shape=[jax.ShapeDtypeStruct((size,), jnp.float32), jax.ShapeDtypeStruct((1,), jnp.float32)],
        in_specs=[vmem],
        out_specs=[vmem, smem],
        compiler_params=own_vmem,
        name="last",
    )(received)
    return (participation, total[0])


def solution(mesh):
    placed = (
        P(("grp", "sub"), None, None),
        P(("grp", "sub")),
        P(("grp", "sub"), None),
        P(("grp", "sub"), None, None),
    )

    return jax.shard_map(local, mesh=mesh, in_specs=placed, out_specs=(P(("grp", "sub")), P()), check_vma=False)
```

```python
import functools
import itertools
import math

import jax
import jax.numpy as jnp
from jax import lax
from jax.experimental import pallas as pl
from jax.experimental.pallas import tpu as pltpu
from jax.sharding import PartitionSpec as P

FIELD = 8


def over(value, by):
    return value >> (by.bit_length() - 1) if by & (by - 1) == 0 else value // by


def rest(value, by):
    return value & (by - 1) if by & (by - 1) == 0 else value % by


class Places:
    def __init__(self, count):
        self.count = count
        self.cycle = 4 if count % 4 == 0 else count
        self.mids = count // self.cycle

    def split(self, place):
        if self.cycle != 4:
            return (place, 0)
        low = rest(place, 2)
        high = over(place, 2 * self.mids)
        turn = 2 * low + high * (3 - 4 * low)
        return (turn, rest(over(place, 2), self.mids))

    def join(self, turn, mid):
        if self.cycle != 4:
            return turn
        return rest(turn, 2) * 2 * self.mids + mid * 2 + rest(over(turn + 1, 2), 2)

    def step(self, place, by):
        turn, mid = self.split(place)
        return self.join(rest(turn + by[0], self.cycle), rest(mid + by[1], self.mids))

    def gap(self, there, here):
        return ((there[0] - here[0]) % self.cycle, (there[1] - here[1]) % self.mids)

    def cover(self):
        steps = sorted(
            itertools.product(range(self.cycle), range(self.mids)),
            key=lambda s: ((s[0] > 0) + (s[1] > 0), s),
        )

        def reached(chosen):
            return {self.gap(a, b) for a in chosen for b in chosen}

        chosen = [(0, 0)]
        while len(reached(chosen)) < self.count:
            chosen.append(max(steps, key=lambda s: len(reached(chosen + [s]))))
        held = sorted(chosen, key=lambda s: (s != (0, 0), s != (2, 0), s))
        pairs = {}
        for (i, row), (j, source) in itertools.product(enumerate(held), enumerate(held)):
            wanted = self.gap(source, row)
            if wanted not in pairs or max(i, j) < max(pairs[wanted]):
                pairs[wanted] = (i, j)
        return held, sorted(pairs.values())


class Plan:
    def __init__(self, groups, subs, width, far_width):
        self.groups = groups
        self.subs = subs
        self.listed = width // groups
        self.named = far_width // groups
        self.places = Places(groups)
        self.held, self.pairs = self.places.cover()
        self.steps = list(itertools.product(range(self.places.cycle), range(self.places.mids)))
        self.near = 2 if (2, 0) in self.held and len(self.held) > 2 else 1
        self.order = sorted(range(len(self.held)), key=lambda i: (self.held[i] == (2, 0), i))

    def owner(self, i):
        return self.places.step(lax.axis_index("grp"), self.held[i]) * self.subs + lax.axis_index("sub")

    def at(self, i, j):
        return self.steps.index(self.places.gap(self.held[j], self.held[i]))


def pack_kernel(plan, pair_lists, far_slots, block_cols, raw, meta, strict, kept, by_group):
    groups, listed, named = plan.groups, plan.listed, plan.named
    stored, size = raw.shape[:2]
    left, place, mask, live = (pair_lists[0, field : field + 1] for field in range(4))
    width = place.shape[1]
    spread = lax.broadcasted_iota(jnp.int32, (groups * named, width), 0)
    source = lax.broadcasted_iota(jnp.int32, (groups * named, width), 1) // listed
    wanted = (spread == source * named + place).astype(jnp.float32)
    slots = jnp.broadcast_to(far_slots[...].astype(jnp.float32), (8, groups * named))
    far = jnp.dot(slots, wanted, preferred_element_type=jnp.float32)[:1].astype(jnp.int32)
    codes = left + far * 2**FIELD + jnp.where(live == 1, mask, stored) * 4**FIELD
    for group in range(groups):
        by_group[group, :, :listed] = codes[:, group * listed : (group + 1) * listed]
    for at, step in enumerate(plan.steps):
        meta[at] = by_group[plan.places.step(lax.axis_index("grp"), step)]
    for slot in range(stored):
        meta[groups + slot] = jnp.full((1, size), block_cols[slot] != plan.owner(0), meta.dtype)
    rows = lax.broadcasted_iota(jnp.int32, (size, size), 0)
    columns = lax.broadcasted_iota(jnp.int32, (size, size), 1)
    strict[...] = (rows > columns).astype(jnp.float32).astype(strict.dtype)
    keep_strict(groups, raw, meta, strict, kept)


def keep_strict(groups, raw, meta, strict, kept, wide=None):
    stored = raw.shape[0]
    for slot in range(stored):
        off_diag = meta[groups + slot].astype(jnp.float32).astype(kept.dtype)
        kept[slot] = raw[slot] * jnp.maximum(strict[...], off_diag)
        if wide is not None:
            wide[slot] = kept[slot].astype(wide.dtype)
    kept[stored] = jnp.zeros_like(kept[stored])
    if wide is not None:
        wide[stored] = jnp.zeros_like(wide[stored])


def add_triples(plan, acc, row, masks, source, codes):
    field = 2**FIELD - 1
    for w in range(plan.listed):
        code = codes[0, w]
        left = row[code & field]
        far = source[(code >> FIELD) & field]
        mask = masks[code >> (2 * FIELD)]
        acc = acc + mask.astype(jnp.float32) * jnp.dot(left, far, preferred_element_type=jnp.float32)
    return acc


def stage_kernel(plan, first, last, new, pairs, *refs):
    refs = list(refs)
    strict = refs.pop(0)
    metas = [refs.pop(0) for _ in range(new.stop)]
    kept = [refs.pop(0) for _ in range(new.start)]
    raws = [refs.pop(0) for _ in new]
    before = None if first else refs.pop(0)
    if not last:
        kept += [refs.pop(0) for _ in new]
    out = refs.pop(0)
    if last:
        kept += [refs.pop(0) for _ in new]

    for i in new:
        keep_strict(plan.groups, raws[i - new.start], metas[i], strict, kept[i])
    size = kept[0].shape[1]
    done = 0 if first else new.start
    sums = {}
    for i in range(new.stop):
        acc = before[i] if i < done else jnp.zeros((size, size), jnp.float32)
        for row, j in pairs:
            if row == i:
                acc = add_triples(plan, acc, kept[i], kept[i], kept[j], metas[i][plan.at(i, j)])
        if last:
            sums[i] = jnp.sum(acc.T, axis=0, keepdims=True)
        else:
            out[i] = acc
    if not last:
        return
    out[:, :, :size] = jnp.zeros((out.shape[0], 1, size), out.dtype)
    out[:, :, size:] = jnp.broadcast_to(sum(sums.values())[None], (out.shape[0], 1, size))
    for i, vector in sums.items():
        out[plan.owner(i), :, :size] = vector


def last_kernel(divisor, received, participation, total):
    size = participation.shape[0]
    summed = jnp.sum(received[:, 0, :], axis=0, keepdims=True)
    participation[...] = summed[0, :size]
    total[0] = jnp.sum(summed[:, size:]) / divisor


def in_vmem(array):
    return pltpu.with_memory_space_constraint(array, pltpu.VMEM)


def local(blocks, block_cols, far_slots, pair_lists):
    stored, size = blocks.shape[:2]
    groups = lax.axis_size("grp")
    subs = lax.axis_size("sub")
    width = pair_lists.shape[2]
    far_width = far_slots.shape[1]
    plan = Plan(groups, subs, width, far_width)
    held = plan.held

    def brought(array, i):
        if i == 0:
            return array
        pairs = [(plan.places.step(g, held[i]), g) for g in range(groups)]
        return lax.ppermute(array, "grp", pairs)

    raws = {i: brought(blocks, i) for i in plan.order}
    kept_shape = (stored + 1, size, size)
    own_vmem = pltpu.CompilerParams(vmem_limit_bytes=16 * 2**20)
    smem = pl.BlockSpec(memory_space=pltpu.SMEM)
    vmem = pl.BlockSpec(memory_space=pltpu.VMEM)
    meta, strict, own = pl.pallas_call(
        functools.partial(pack_kernel, plan),
        out_shape=[
            pltpu.VMEM((groups + stored, 1, size), jnp.int32),
            pltpu.VMEM((size, size), blocks.dtype),
            pltpu.VMEM(kept_shape, blocks.dtype),
        ],
        in_specs=[vmem, vmem, smem, vmem],
        out_specs=[vmem, vmem, vmem],
        scratch_shapes=[pltpu.VMEM((groups, 1, size), jnp.int32)],
        compiler_params=own_vmem,
        name="pack",
    )(*(pltpu.with_memory_space_constraint(a, pltpu.HBM) for a in (pair_lists, far_slots, block_cols, blocks)))
    metas = {i: brought(meta, i) for i in plan.order}

    stages = [range(1, plan.near)] + [range(i, i + 1) for i in range(plan.near, len(held))]
    kept = [own]
    sums = []
    for at, new in enumerate(stages):
        first, last = at == 0, at == len(stages) - 1
        pairs = [p for p in plan.pairs if max(p) in new or first and max(p) == 0]
        if last:
            out_shape = pltpu.VMEM((groups * subs, 1, 2 * size), jnp.float32)
        else:
            out_shape = [pltpu.VMEM(kept_shape, blocks.dtype)] * len(new)
            out_shape += [pltpu.VMEM((new.stop, size, size), jnp.float32)]
        operands = [in_vmem(a) for a in [strict] + [metas[i] for i in range(new.stop)] + kept + [raws[i] for i in new] + sums]
        call = pl.pallas_call(
            functools.partial(stage_kernel, plan, first, last, new, pairs),
            out_shape=out_shape,
            in_specs=[vmem] * len(operands),
            out_specs=vmem if last else [vmem] * (len(new) + 1),
            scratch_shapes=[pltpu.VMEM(kept_shape, blocks.dtype)] * len(new) if last else [],
            cost_estimate=pl.CostEstimate(
                flops=len(pairs) * plan.listed * 2 * size**3,
                bytes_accessed=2 * len(new) * stored * size * size * blocks.dtype.itemsize,
                transcendentals=0,
            ),
            compiler_params=own_vmem,
        )
        out = call(*operands)
        if not last:
            kept += out[:-1]
            sums = [out[-1]]
    received = in_vmem(lax.all_to_all(out, ("grp", "sub"), split_axis=0, concat_axis=0, tiled=True))
    participation, total = pl.pallas_call(
        functools.partial(last_kernel, math.sqrt(groups * subs * size)),
        out_shape=[jax.ShapeDtypeStruct((size,), jnp.float32), jax.ShapeDtypeStruct((1,), jnp.float32)],
        in_specs=[vmem],
        out_specs=[vmem, smem],
        compiler_params=own_vmem,
        name="last",
    )(received)
    return (participation, total[0])


def solution(mesh):
    placed = (
        P(("grp", "sub"), None, None),
        P(("grp", "sub")),
        P(("grp", "sub"), None),
        P(("grp", "sub"), None, None),
    )

    return jax.shard_map(local, mesh=mesh, in_specs=placed, out_specs=(P(("grp", "sub")), P()), check_vma=False)
```

```python
import functools
import itertools
import math

import jax
import jax.numpy as jnp
from jax import lax
from jax.experimental import pallas as pl
from jax.experimental.pallas import tpu as pltpu
from jax.sharding import PartitionSpec as P

FIRST = -1
FIELD = 8


class Places:
    def __init__(self, count):
        self.count = count
        self.chips = count // 2
        self.paired = count % 2 == 0 and self.chips & (self.chips - 1) == 0

    def split(self, place):
        if not self.paired:
            return place
        turn = place >> 1
        shift = 1
        while shift < self.chips:
            turn = turn ^ (turn >> shift)
            shift *= 2
        return turn + (place & 1) * self.chips

    def step(self, place, by):
        turn = self.split(place) + by
        if not self.paired:
            return turn % self.count
        turn = turn & (self.count - 1)
        chip = turn & (self.chips - 1)
        return (chip ^ (chip >> 1)) * 2 + (turn >> (self.chips.bit_length() - 1))

    def gap(self, there, here):
        return (there - here) % self.count

    def cover(self):
        def reached(chosen):
            return {self.gap(a, b) for a in chosen for b in chosen}

        held = [0]
        for step in (self.chips, FIRST % self.count, -FIRST % self.count):
            if step not in held and len(reached(held)) < self.count:
                held.append(step)
        while len(reached(held)) < self.count:
            held.append(max(range(self.count), key=lambda s: len(reached(held + [s]))))
        pairs = {}
        for (i, row), (j, source) in itertools.product(enumerate(held), enumerate(held)):
            wanted = self.gap(source, row)
            if wanted not in pairs or max(i, j) < max(pairs[wanted]):
                pairs[wanted] = (i, j)
        return held, sorted(pairs.values())


class Plan:
    def __init__(self, groups, subs, width, far_width):
        self.groups = groups
        self.subs = subs
        self.listed = width // groups
        self.named = far_width // groups
        self.places = Places(groups)
        self.held, self.pairs = self.places.cover()
        self.near = min(2, len(self.held) - 1)
        self.order = [0] + list(range(self.near, len(self.held))) + list(range(1, self.near))

    def owner(self, i):
        return self.places.step(lax.axis_index("grp"), self.held[i]) * self.subs + lax.axis_index("sub")

    def at(self, i, j):
        return self.places.gap(self.held[j], self.held[i])


def pack_kernel(plan, pair_lists, far_slots, block_cols, raw, meta, strict, kept, by_group):
    groups, listed, named = plan.groups, plan.listed, plan.named
    stored, size = raw.shape[:2]
    left, place, mask, live = (pair_lists[0, field : field + 1] for field in range(4))
    width = place.shape[1]
    spread = lax.broadcasted_iota(jnp.int32, (groups * named, width), 0)
    source = lax.broadcasted_iota(jnp.int32, (groups * named, width), 1) // listed
    wanted = (spread == source * named + place).astype(jnp.float32)
    slots = jnp.broadcast_to(far_slots[...].astype(jnp.float32), (8, groups * named))
    far = jnp.dot(slots, wanted, preferred_element_type=jnp.float32)[:1].astype(jnp.int32)
    codes = left + far * 2**FIELD + jnp.where(live == 1, mask, stored) * 4**FIELD
    for group in range(groups):
        by_group[group, :, :listed] = codes[:, group * listed : (group + 1) * listed]
    for step in range(groups):
        meta[step] = by_group[plan.places.step(lax.axis_index("grp"), step)]
    for slot in range(stored):
        meta[groups + slot] = jnp.full((1, size), block_cols[slot] != plan.owner(0), meta.dtype)
    rows = lax.broadcasted_iota(jnp.int32, (size, size), 0)
    columns = lax.broadcasted_iota(jnp.int32, (size, size), 1)
    strict[...] = (rows > columns).astype(jnp.float32).astype(strict.dtype)
    keep_strict(groups, raw, meta, strict, kept)


def keep_strict(groups, raw, meta, strict, kept, wide=None):
    stored = raw.shape[0]
    for slot in range(stored):
        off_diag = meta[groups + slot].astype(jnp.float32).astype(kept.dtype)
        kept[slot] = raw[slot] * jnp.maximum(strict[...], off_diag)
        if wide is not None:
            wide[slot] = kept[slot].astype(wide.dtype)
    kept[stored] = jnp.zeros_like(kept[stored])
    if wide is not None:
        wide[stored] = jnp.zeros_like(wide[stored])


def add_triples(plan, acc, row, masks, source, codes):
    field = 2**FIELD - 1
    for w in range(plan.listed):
        code = codes[0, w]
        left = row[code & field]
        far = source[(code >> FIELD) & field]
        mask = masks[code >> (2 * FIELD)]
        acc = acc + mask.astype(jnp.float32) * jnp.dot(left, far, preferred_element_type=jnp.float32)
    return acc


def stage_kernel(plan, first, last, new, pairs, *refs):
    refs = list(refs)
    strict = refs.pop(0)
    metas = [refs.pop(0) for _ in range(new.stop)]
    kept = [refs.pop(0) for _ in range(new.start)]
    raws = [refs.pop(0) for _ in new]
    before = None if first else refs.pop(0)
    if not last:
        kept += [refs.pop(0) for _ in new]
    out = refs.pop(0)
    if last:
        kept += [refs.pop(0) for _ in new]

    for i in new:
        keep_strict(plan.groups, raws[i - new.start], metas[i], strict, kept[i])
    size = kept[0].shape[1]
    done = 0 if first else new.start
    sums = {}
    for i in range(new.stop):
        acc = before[i] if i < done else jnp.zeros((size, size), jnp.float32)
        for row, j in pairs:
            if row == i:
                acc = add_triples(plan, acc, kept[i], kept[i], kept[j], metas[i][plan.at(i, j)])
        if last:
            sums[i] = jnp.sum(acc.T, axis=0, keepdims=True)
        else:
            out[i] = acc
    if not last:
        return
    out[:, :, :size] = jnp.zeros((out.shape[0], 1, size), out.dtype)
    out[:, :, size:] = jnp.broadcast_to(sum(sums.values())[None], (out.shape[0], 1, size))
    for i, vector in sums.items():
        out[plan.owner(i), :, :size] = vector


def last_kernel(divisor, received, participation, total):
    size = participation.shape[0]
    summed = jnp.sum(received[:, 0, :], axis=0, keepdims=True)
    participation[...] = summed[0, :size]
    total[...] = (jnp.sum(summed[:, size:], axis=1, keepdims=True) / divisor)[0]


def in_vmem(array):
    return pltpu.with_memory_space_constraint(array, pltpu.VMEM)


def local(blocks, block_cols, far_slots, pair_lists):
    stored, size = blocks.shape[:2]
    groups = lax.axis_size("grp")
    subs = lax.axis_size("sub")
    width = pair_lists.shape[2]
    far_width = far_slots.shape[1]
    plan = Plan(groups, subs, width, far_width)
    held = plan.held

    def brought(array, i):
        if i == 0:
            return array
        pairs = [(plan.places.step(g, held[i]), g) for g in range(groups)]
        return lax.ppermute(array, "grp", pairs)

    raws = {i: brought(blocks, i) for i in plan.order}
    kept_shape = (stored + 1, size, size)
    own_vmem = pltpu.CompilerParams(vmem_limit_bytes=16 * 2**20)
    smem = pl.BlockSpec(memory_space=pltpu.SMEM)
    vmem = pl.BlockSpec(memory_space=pltpu.VMEM)
    meta, strict, own = pl.pallas_call(
        functools.partial(pack_kernel, plan),
        out_shape=[
            pltpu.VMEM((groups + stored, 1, size), jnp.int32),
            pltpu.VMEM((size, size), blocks.dtype),
            pltpu.VMEM(kept_shape, blocks.dtype),
        ],
        in_specs=[vmem, vmem, smem, vmem],
        out_specs=[vmem, vmem, vmem],
        scratch_shapes=[pltpu.VMEM((groups, 1, size), jnp.int32)],
        compiler_params=own_vmem,
        name="pack",
    )(*(pltpu.with_memory_space_constraint(a, pltpu.HBM) for a in (pair_lists, far_slots, block_cols, blocks)))
    metas = {i: brought(meta, i) for i in plan.order}

    stages = [range(1, plan.near)] + [range(i, i + 1) for i in range(plan.near, len(held))]
    kept = [own]
    sums = []
    for at, new in enumerate(stages):
        first, last = at == 0, at == len(stages) - 1
        pairs = [p for p in plan.pairs if max(p) in new or first and max(p) == 0]
        if last:
            out_shape = pltpu.VMEM((groups * subs, 1, 2 * size), jnp.float32)
        else:
            out_shape = [pltpu.VMEM(kept_shape, blocks.dtype)] * len(new)
            out_shape += [pltpu.VMEM((new.stop, size, size), jnp.float32)]
        operands = [in_vmem(a) for a in [strict] + [metas[i] for i in range(new.stop)] + kept + [raws[i] for i in new] + sums]
        call = pl.pallas_call(
            functools.partial(stage_kernel, plan, first, last, new, pairs),
            out_shape=out_shape,
            in_specs=[vmem] * len(operands),
            out_specs=vmem if last else [vmem] * (len(new) + 1),
            scratch_shapes=[pltpu.VMEM(kept_shape, blocks.dtype)] * len(new) if last else [],
            cost_estimate=pl.CostEstimate(
                flops=len(pairs) * plan.listed * 2 * size**3,
                bytes_accessed=2 * len(new) * stored * size * size * blocks.dtype.itemsize,
                transcendentals=0,
            ),
            compiler_params=own_vmem,
        )
        out = call(*operands)
        if not last:
            kept += out[:-1]
            sums = [out[-1]]
    received = in_vmem(lax.all_to_all(out, ("grp", "sub"), split_axis=0, concat_axis=0, tiled=True))
    participation, total = pl.pallas_call(
        functools.partial(last_kernel, math.sqrt(groups * subs * size)),
        out_shape=[jax.ShapeDtypeStruct((size,), jnp.float32), jax.ShapeDtypeStruct((1,), jnp.float32)],
        in_specs=[vmem],
        out_specs=[vmem, vmem],
        compiler_params=own_vmem,
        name="last",
    )(received)
    return (participation, total[0])


def solution(mesh):
    placed = (
        P(("grp", "sub"), None, None),
        P(("grp", "sub")),
        P(("grp", "sub"), None),
        P(("grp", "sub"), None, None),
    )

    return jax.shard_map(local, mesh=mesh, in_specs=placed, out_specs=(P(("grp", "sub")), P()), check_vma=False)
```

```python
import functools
import itertools
import math

import jax
import jax.numpy as jnp
from jax import lax
from jax.experimental import pallas as pl
from jax.experimental.pallas import tpu as pltpu
from jax.sharding import PartitionSpec as P

FIRST = -1
FIELD = 8


class Places:
    def __init__(self, count):
        self.count = count
        self.chips = count // 2
        self.paired = count % 2 == 0 and self.chips & (self.chips - 1) == 0

    def split(self, place):
        if not self.paired:
            return place
        turn = place >> 1
        shift = 1
        while shift < self.chips:
            turn = turn ^ (turn >> shift)
            shift *= 2
        return turn + (place & 1) * self.chips

    def step(self, place, by):
        turn = self.split(place) + by
        if not self.paired:
            return turn % self.count
        turn = turn & (self.count - 1)
        chip = turn & (self.chips - 1)
        return (chip ^ (chip >> 1)) * 2 + (turn >> (self.chips.bit_length() - 1))

    def gap(self, there, here):
        return (there - here) % self.count

    def cover(self):
        def reached(chosen):
            return {self.gap(a, b) for a in chosen for b in chosen}

        held = [0]
        for step in (self.chips, FIRST % self.count, -FIRST % self.count):
            if step not in held and len(reached(held)) < self.count:
                held.append(step)
        while len(reached(held)) < self.count:
            held.append(max(range(self.count), key=lambda s: len(reached(held + [s]))))
        pairs = {}
        for (i, row), (j, source) in itertools.product(enumerate(held), enumerate(held)):
            wanted = self.gap(source, row)
            if wanted not in pairs or max(i, j) < max(pairs[wanted]):
                pairs[wanted] = (i, j)
        return held, sorted(pairs.values())


class Plan:
    def __init__(self, groups, subs, width, far_width, size):
        self.groups = groups
        self.subs = subs
        self.listed = width // groups
        self.named = far_width // groups
        self.per_row = max(1, size // self.listed)
        self.rows = -(-groups // self.per_row)
        self.places = Places(groups)
        self.held, self.pairs = self.places.cover()
        self.near = min(2, len(self.held) - 1)
        self.order = [0] + list(range(self.near, len(self.held))) + list(range(1, self.near))

    def owner(self, i):
        return self.places.step(lax.axis_index("grp"), self.held[i]) * self.subs + lax.axis_index("sub")

    def spot(self, step):
        return step // self.per_row, step % self.per_row * self.listed

    def codes(self, meta, i, j):
        row, lane = self.spot(self.places.gap(self.held[j], self.held[i]))
        left, mask, far = (meta[field * self.rows + row] for field in range(3))
        codes = left + mask * 2**FIELD + far * 4**FIELD
        return [codes[0, lane + w] for w in range(self.listed)]


def pack_kernel(plan, pair_lists, far_slots, block_cols, raw, meta, strict, kept, by_group, by_step):
    groups, listed, named = plan.groups, plan.listed, plan.named
    stored, size = raw.shape[:2]
    left, place, mask, live = (pair_lists[0, field : field + 1] for field in range(4))
    width = place.shape[1]
    spread = lax.broadcasted_iota(jnp.int32, (groups * named, width), 0)
    source = lax.broadcasted_iota(jnp.int32, (groups * named, width), 1) // listed
    wanted = (spread == source * named + place).astype(jnp.float32)
    slots = jnp.broadcast_to(far_slots[...].astype(jnp.float32), (8, groups * named))
    far = jnp.dot(slots, wanted, preferred_element_type=jnp.float32)[:1].astype(jnp.int32)
    codes = left + jnp.where(live == 1, mask, stored) * 2**FIELD + far * 4**FIELD
    for group in range(groups):
        by_group[group, :, :listed] = codes[:, group * listed : (group + 1) * listed]
    for step in range(groups):
        row, lane = plan.spot(step)
        group = plan.places.step(lax.axis_index("grp"), step)
        by_step[row, :, lane : lane + listed] = by_group[group, :, :listed]
    for row in range(plan.rows):
        for field in range(3):
            meta[field * plan.rows + row] = (by_step[row] >> (field * FIELD)) & (2**FIELD - 1)
    for slot in range(stored):
        meta[3 * plan.rows + slot] = jnp.full((1, size), block_cols[slot] != plan.owner(0), meta.dtype)
    rows = lax.broadcasted_iota(jnp.int32, (size, size), 0)
    columns = lax.broadcasted_iota(jnp.int32, (size, size), 1)
    strict[...] = (rows > columns).astype(jnp.float32).astype(strict.dtype)
    keep_strict(plan, raw, meta, strict, kept)


def keep_strict(plan, raw, meta, strict, kept):
    stored = raw.shape[0]
    for slot in range(stored):
        off_diag = meta[3 * plan.rows + slot].astype(jnp.float32).astype(kept.dtype)
        kept[slot] = raw[slot] * jnp.maximum(strict[...], off_diag)
    kept[stored] = jnp.zeros_like(kept[stored])


def add_triples(acc, row, source, codes):
    field = 2**FIELD - 1
    for code in codes:
        left = row[code & field]
        mask = row[(code >> FIELD) & field]
        far = source[code >> (2 * FIELD)]
        acc = acc + mask.astype(jnp.float32) * jnp.dot(left, far, preferred_element_type=jnp.float32)
    return acc


def stage_kernel(plan, first, last, new, pairs, *refs):
    refs = list(refs)
    strict = refs.pop(0)
    metas = [refs.pop(0) for _ in range(new.stop)]
    kept = [refs.pop(0) for _ in range(new.start)]
    raws = [refs.pop(0) for _ in new]
    before = None if first else refs.pop(0)
    if not last:
        kept += [refs.pop(0) for _ in new]
    out = refs.pop(0)
    if last:
        kept += [refs.pop(0) for _ in new]

    for i in new:
        keep_strict(plan, raws[i - new.start], metas[i], strict, kept[i])
    size = kept[0].shape[1]
    done = 0 if first else new.start
    sums = {}
    for i in range(new.stop):
        acc = before[i] if i < done else jnp.zeros((size, size), jnp.float32)
        for row, j in pairs:
            if row == i:
                acc = add_triples(acc, kept[i], kept[j], plan.codes(metas[i], i, j))
        if last:
            sums[i] = jnp.sum(acc.T, axis=0, keepdims=True)
        else:
            out[i] = acc
    if not last:
        return
    out[:, :, :size] = jnp.zeros((out.shape[0], 1, size), out.dtype)
    out[:, :, size:] = jnp.broadcast_to(sum(sums.values())[None], (out.shape[0], 1, size))
    for i, vector in sums.items():
        out[plan.owner(i), :, :size] = vector


def last_kernel(divisor, received, participation, total):
    size = participation.shape[0]
    summed = jnp.sum(received[:, 0, :], axis=0, keepdims=True)
    participation[...] = summed[0, :size]
    total[...] = (jnp.sum(summed[:, size:], axis=1, keepdims=True) / divisor)[0]


def in_vmem(array):
    return pltpu.with_memory_space_constraint(array, pltpu.VMEM)


def local(blocks, block_cols, far_slots, pair_lists):
    stored, size = blocks.shape[:2]
    groups = lax.axis_size("grp")
    subs = lax.axis_size("sub")
    width = pair_lists.shape[2]
    far_width = far_slots.shape[1]
    plan = Plan(groups, subs, width, far_width, size)
    held = plan.held

    def brought(array, i):
        if i == 0:
            return array
        pairs = [(plan.places.step(g, held[i]), g) for g in range(groups)]
        return lax.ppermute(array, "grp", pairs)

    raws = {i: brought(blocks, i) for i in plan.order}
    kept_shape = (stored + 1, size, size)
    own_vmem = pltpu.CompilerParams(vmem_limit_bytes=16 * 2**20)
    even = pltpu.CompilerParams(vmem_limit_bytes=own_vmem.vmem_limit_bytes)
    smem = pl.BlockSpec(memory_space=pltpu.SMEM)
    vmem = pl.BlockSpec(memory_space=pltpu.VMEM)
    meta, strict, own = pl.pallas_call(
        functools.partial(pack_kernel, plan),
        out_shape=[
            pltpu.VMEM((3 * plan.rows + stored, 1, size), jnp.int32),
            pltpu.VMEM((size, size), blocks.dtype),
            pltpu.VMEM(kept_shape, blocks.dtype),
        ],
        in_specs=[vmem, vmem, smem, vmem],
        out_specs=[vmem, vmem, vmem],
        scratch_shapes=[pltpu.VMEM((rows, 1, size), jnp.int32) for rows in (groups, plan.rows)],
        compiler_params=own_vmem,
        name="pack",
    )(*(pltpu.with_memory_space_constraint(a, pltpu.HBM) for a in (pair_lists, far_slots, block_cols, blocks)))
    metas = {i: brought(meta, i) for i in plan.order}

    stages = [range(1, plan.near)] + [range(i, i + 1) for i in range(plan.near, len(held))]
    kept = [own]
    sums = []
    for at, new in enumerate(stages):
        first, last = at == 0, at == len(stages) - 1
        pairs = [p for p in plan.pairs if max(p) in new or first and max(p) == 0]
        if last:
            out_shape = pltpu.VMEM((groups * subs, 1, 2 * size), jnp.float32)
        else:
            out_shape = [pltpu.VMEM(kept_shape, blocks.dtype)] * len(new)
            out_shape += [pltpu.VMEM((new.stop, size, size), jnp.float32)]
        operands = [in_vmem(a) for a in [strict] + [metas[i] for i in range(new.stop)] + kept + [raws[i] for i in new] + sums]
        call = pl.pallas_call(
            functools.partial(stage_kernel, plan, first, last, new, pairs),
            out_shape=out_shape,
            in_specs=[vmem] * len(operands),
            out_specs=vmem if last else [vmem] * (len(new) + 1),
            scratch_shapes=[pltpu.VMEM(kept_shape, blocks.dtype)] * len(new) if last else [],
            cost_estimate=pl.CostEstimate(
                flops=len(pairs) * plan.listed * 2 * size**3,
                bytes_accessed=2 * len(new) * stored * size * size * blocks.dtype.itemsize,
                transcendentals=0,
            ),
            compiler_params=own_vmem if last else even,
        )
        out = call(*operands)
        if not last:
            kept += out[:-1]
            sums = [out[-1]]
    received = in_vmem(lax.all_to_all(out, ("grp", "sub"), split_axis=0, concat_axis=0, tiled=True))
    participation, total = pl.pallas_call(
        functools.partial(last_kernel, math.sqrt(groups * subs * size)),
        out_shape=[jax.ShapeDtypeStruct((size,), jnp.float32), jax.ShapeDtypeStruct((1,), jnp.float32)],
        in_specs=[vmem],
        out_specs=[vmem, vmem],
        compiler_params=own_vmem,
        name="last",
    )(received)
    return (participation, total[0])


def solution(mesh):
    placed = (
        P(("grp", "sub"), None, None),
        P(("grp", "sub")),
        P(("grp", "sub"), None),
        P(("grp", "sub"), None, None),
    )

    return jax.shard_map(local, mesh=mesh, in_specs=placed, out_specs=(P(("grp", "sub")), P()), check_vma=False)
```
